32 devices in a mesh: wide: 16 (over z, y, core), narrow: 2 (over x).
Axes of the slice: x: 2, y: 2, z: 4, core: 2. Of those that a mesh axis runs over, the one named last changes fastest.
Arguments:
- enc_hidden: bfloat16 [3072, 6144], P('wide', 'narrow'), may hold values from -6 to 6
- enc_gain: float32 [6144], P('narrow'), may hold values from 0.1 to 1.9
- cross_weight: bfloat16 [6144, 256], P('narrow'), may hold values from -0.078125 to 0.078125
- assign: int32 [16], P('wide'), may hold values from 0 to 1
- token_ids: int32 [16, 2, 64], P('wide'), may hold values from 0 to 7999, as said below
- cross_table: bfloat16 [8000, 6144], P('wide', 'narrow'), may hold values from -540 to 540
- self_table: bfloat16 [8000, 6144], P('wide', 'narrow'), may hold values from -540 to 540
- kv_table: bfloat16 [8000, 256], P('wide'), may hold values from -6 to 6
- self_cache: bfloat16 [16, 64, 768, 256], P('wide', 'narrow'), may hold values from -6 to 6
Outputs:
- cross_out: bfloat16 [16, 2, 64, 6144], P('wide', None, None, 'narrow')
- self_out: bfloat16 [16, 2, 64, 6144], P('wide', None, 'narrow')
The draws below stay inside these ranges and needn't reach their ends.
Inputs may be any that keep to these rules, and one draw needn't show every extreme that they name: `token_ids`: within one group, at most 16 of its 128 ids lie in any one of the 16 ranges of 500 consecutive ids, and some range holds exactly 16 of them.
All inputs are finite; a program needn't handle non-finite values.
Results may differ from the reference program's by a relative error of at most 0.009.
The reference program's roundings to bfloat16 on the way count: a program that leaves them out, or rounds other values in their place, can miss the bound.
Values may be sent and summed in bfloat16 or wider, within the bound.
A program may use at most 128 MiB of HBM per device.

```python
import jax
import jax.numpy as jnp
from jax import lax

D = 6144
HEADS = 48
HEAD = 128
VOCAB = 8000
STEPS = 2
ENC_LEN = 1536
CAND = 64
PREFIX = 768
PROBLEMS = 2
GROUPS = 16
ENC_ROWS = 3072
CAP = 16


def draw_token_ids(key, part):
    slots = GROUPS * CAP
    per_owner = VOCAB // GROUPS
    heavy = jax.random.randint(jax.random.fold_in(key, 11), (), 0, GROUPS)

    def one_group(group_key):
        order_key = jax.random.fold_in(group_key, 1)
        shuffle_key = jax.random.fold_in(group_key, 2)
        local_key = jax.random.fold_in(group_key, 3)
        order = jax.random.permutation(order_key, slots)
        owner = order // CAP
        score = jnp.where(owner == heavy, 0, 1) * slots + jnp.arange(slots)
        picked = jnp.argsort(score)[:STEPS * CAND]
        owners = jax.random.permutation(shuffle_key, owner[picked])
        local = jax.random.randint(local_key, (STEPS * CAND,), 0, per_owner)
        return (owners * per_owner + local).astype(jnp.int32).reshape(STEPS, CAND)
    group_keys = jax.random.split(jax.random.fold_in(key, 12), GROUPS)
    return jax.vmap(one_group)(group_keys)


def draw_cross_table(key, part):
    base = jnp.clip(jax.random.normal(jax.random.fold_in(key, 21), (VOCAB, HEADS * HEAD), jnp.float32), -6.0, 6.0) * 3.0
    return base.astype(jnp.bfloat16)


def draw_self_table(key, part):
    base = jnp.clip(jax.random.normal(jax.random.fold_in(key, 31), (VOCAB, HEADS * HEAD), jnp.float32), -6.0, 6.0) * 3.0
    return base.astype(jnp.bfloat16)


def plant(values, rng, low, top_value):
    shape = values.shape
    index_at = [jax.random.randint(jax.random.fold_in(rng, axis), (), 0, shape[axis]) for axis in range(len(shape))]
    values = values.at[tuple(index_at)].set(low)
    longest = shape.index(max(shape))
    index_at[longest] = (index_at[longest] + 1) % shape[longest]
    return values.at[tuple(index_at)].set(top_value)


def block_scale(own_key, shape, cuts, smallest, top_value):
    def one(dim, parts):
        draws = jax.random.uniform(jax.random.fold_in(jax.random.fold_in(own_key, 6), dim), (parts,), jnp.float32, smallest / len(cuts), top_value / len(cuts))
        return jnp.repeat(jnp.exp(draws), shape[dim] // parts).reshape((-1,) + (1,) * (len(shape) - dim - 1))

    level = one(*cuts[0])
    for cut in cuts[1:]:
        level = level * one(*cut)
    return level


def bell_draw(key, shape, scale, reach, shards=(), kind=jnp.bfloat16):
    entries = jax.random.normal(key, shape, jnp.float32) * scale
    if len(shards) > 0:
        entries = block_scale(key, shape, shards, -0.22, 0.18) * entries
    return jnp.clip(entries, min=-reach, max=reach).astype(kind)


def setup_inputs(seed: int = 0) -> dict:
    splits = jax.random.split(jax.random.key(seed), 10)
    enc_hidden = bell_draw(splits[0], (ENC_ROWS, D), 1.0, 6.0, ((0, 16), (1, 2)))
    enc_gain = jnp.clip(1.0 + 0.18 * jax.random.normal(splits[1], (D,), jnp.float32), 0.1, 1.9)
    cross_weight = bell_draw(splits[2], (D, 2 * HEAD), D ** -0.5, 0.078125, ((0, 2),))
    assign = plant(jax.random.randint(splits[3], (GROUPS,), 0, PROBLEMS), jax.random.fold_in(splits[3], 1), 0, PROBLEMS - 1).astype(jnp.int32)
    token_ids = draw_token_ids(jax.random.fold_in(splits[9], 71), 0)
    cross_table = draw_cross_table(jax.random.fold_in(splits[9], 71), 0)
    self_table = draw_self_table(jax.random.fold_in(splits[9], 71), 0)
    kv_table = bell_draw(splits[7], (VOCAB, 2 * HEAD), 1.0, 6.0, ((0, 16),))
    self_cache = bell_draw(splits[8], (GROUPS, CAND, PREFIX, 2 * HEAD), 1.0, 6.0, ((0, 16), (1, 2)))
    return dict(enc_hidden=enc_hidden, enc_gain=enc_gain, cross_weight=cross_weight, assign=assign, token_ids=token_ids, cross_table=cross_table, self_table=self_table, kv_table=kv_table, self_cache=self_cache)


EPS = 1e-06

def reference(enc_hidden, enc_gain, cross_weight, assign, token_ids, cross_table, self_table, kv_table, self_cache):
    hidden = enc_hidden.astype(jnp.float32)
    meansq = lax.optimization_barrier(jnp.mean(hidden * hidden, axis=1))
    scaled = (hidden * enc_gain.astype(jnp.float32)).astype(jnp.bfloat16)
    projected = jnp.dot(scaled, cross_weight, preferred_element_type=jnp.float32)
    enc_kv = (projected * lax.rsqrt(meansq + EPS)[:, None]).astype(jnp.bfloat16)
    enc_kv = enc_kv.reshape(PROBLEMS, ENC_LEN, 2 * HEAD)
    factor = HEAD ** (-0.5)

    def one_group(inputs):
        problem, ids, cache = inputs
        problem_kv = lax.dynamic_index_in_dim(enc_kv, problem.astype(jnp.int32), 0, keepdims=False)
        flat = ids.reshape(-1)
        cross_q = jnp.take(cross_table, flat, axis=0).astype(jnp.float32).reshape(STEPS * CAND, HEADS, HEAD)
        keys = problem_kv[:, :HEAD].astype(jnp.float32)
        values = problem_kv[:, HEAD:].astype(jnp.float32)
        scores = jnp.einsum('rhd,kd->rhk', cross_q, keys) * factor
        peak = lax.optimization_barrier(jnp.max(scores, axis=-1, keepdims=True))
        expo = jnp.exp(scores - peak)
        total = lax.optimization_barrier(jnp.sum(expo, axis=-1))
        weights = expo.astype(jnp.bfloat16).astype(jnp.float32)
        result = jnp.einsum('rhk,kd->rhd', weights, values) / total[..., None]
        cross = result.astype(jnp.bfloat16).reshape(STEPS, CAND, HEADS * HEAD)
        self_q = jnp.take(self_table, flat, axis=0).astype(jnp.float32).reshape(STEPS, CAND, HEADS, HEAD)
        new_kv = jnp.take(kv_table, flat, axis=0).reshape(STEPS, CAND, 2 * HEAD)
        all_kv = jnp.concatenate([cache, jnp.transpose(new_kv, (1, 0, 2))], axis=1).astype(jnp.float32)
        self_scores = jnp.einsum('tchd,cpd->tchp', self_q, all_kv[..., :HEAD]) * factor
        position = jnp.arange(PREFIX + STEPS, dtype=jnp.int32)
        step_index = jnp.arange(STEPS, dtype=jnp.int32)
        allowed = (position[None, :] < PREFIX + 1 + step_index[:, None])[:, None, None, :]
        masked = jnp.where(allowed, self_scores, -jnp.inf)
        self_peak = lax.optimization_barrier(jnp.max(masked, axis=-1, keepdims=True))
        self_expo = jnp.where(allowed, jnp.exp(masked - self_peak), 0.0)
        self_total = lax.optimization_barrier(jnp.sum(self_expo, axis=-1))
        self_weights = self_expo.astype(jnp.bfloat16).astype(jnp.float32)
        self_result = jnp.einsum('tchp,cpd->tchd', self_weights, all_kv[..., HEAD:]) / self_total[..., None]
        selfs = self_result.astype(jnp.bfloat16).reshape(STEPS, CAND, HEADS * HEAD)
        return (cross, selfs)
    cross_out, self_out = lax.map(one_group, (assign, token_ids, self_cache))
    return (cross_out, self_out)
```

```python
import functools
import math

import jax
import jax.numpy as jnp
from jax import lax
from jax.experimental import pallas as pl
from jax.experimental.pallas import tpu as pltpu
from jax.sharding import PartitionSpec as P

D = 6144
HEADS = 48
HEAD = 128
ENC_LEN = 1536
EPS = 1e-06
TILE_ROWS = 16
SCALE = HEAD ** (-0.5) * math.log2(math.e)

MESH_ID = pl.DeviceIdType.MESH
DOT_T = (((1,), (1,)), ((), ()))


def greet(wide, narrow):
    me = lax.axis_index("wide")
    side = lax.axis_index("narrow")
    barrier = pltpu.get_barrier_semaphore()

    @pl.loop(1, wide)
    def _(step):
        pl.semaphore_signal(
            barrier, inc=1, device_id={"wide": lax.rem(me + step, wide)}, device_id_type=MESH_ID
        )

    for step in range(1, narrow):
        pl.semaphore_signal(
            barrier,
            inc=1,
            device_id={"narrow": lax.rem(side + step, narrow)},
            device_id_type=MESH_ID,
        )
    pl.semaphore_wait(barrier, wide + narrow - 2)


def exchange_kernel(
    wide, narrow, ids_ref, part_ref, ids_out, parts_out, id_send, id_recv, part_send, part_recv
):
    me = lax.axis_index("wide")
    side = lax.axis_index("narrow")
    greet(wide, narrow)

    def ids_copy(step):
        return pltpu.make_async_remote_copy(
            src_ref=ids_ref,
            dst_ref=ids_out.at[me],
            send_sem=id_send.at[step],
            recv_sem=id_recv.at[step],
            device_id={"wide": lax.rem(me + step, wide)},
            device_id_type=MESH_ID,
        )

    def part_copy(step):
        return pltpu.make_async_remote_copy(
            src_ref=part_ref,
            dst_ref=parts_out.at[step - 1],
            send_sem=part_send.at[step],
            recv_sem=part_recv.at[step],
            device_id={"narrow": lax.rem(side + step, narrow)},
            device_id_type=MESH_ID,
        )

    @pl.loop(1, wide)
    def _(step):
        ids_copy(step).start()

    for step in range(1, narrow):
        part_copy(step).start()
    ids_out[me] = ids_ref[...]

    @pl.loop(1, wide)
    def _(step):
        ids_copy(step).wait()

    for step in range(1, narrow):
        part_copy(step).wait()


def exchange(ids, part, wide, narrow):
    vmem = pl.BlockSpec(memory_space=pltpu.VMEM)
    return pl.pallas_call(
        functools.partial(exchange_kernel, wide, narrow),
        out_shape=(
            jax.ShapeDtypeStruct((wide,) + ids.shape, ids.dtype),
            jax.ShapeDtypeStruct((narrow - 1,) + part.shape, part.dtype),
        ),
        in_specs=[vmem, vmem],
        out_specs=(vmem, vmem),
        scratch_shapes=[
            pltpu.SemaphoreType.DMA((wide,)),
            pltpu.SemaphoreType.DMA((wide,)),
            pltpu.SemaphoreType.DMA((narrow,)),
            pltpu.SemaphoreType.DMA((narrow,)),
        ],
        compiler_params=pltpu.CompilerParams(collective_id=0, has_side_effects=True),
    )(ids, part)


def main_kernel(
    dims,
    problem_ref,
    enc_ref,
    cross_ref,
    self_ref,
    kv_ref,
    cache_ref,
    perm_cross_ref,
    perm_self_ref,
    cross_out,
    self_out,
    enc_buf,
    keys,
    cross_raw,
    self_raw,
    kv_raw,
    cache,
    fresh,
    q_rows,
    o_rows,
    local_sem,
    enc_send,
    enc_recv,
    self_send,
    self_recv,
    kv_send,
    kv_recv,
    cross_send,
    cross_recv,
    side_send,
    side_recv,
):
    wide, narrow, steps, own, problems, chunks = dims
    me = lax.axis_index("wide")
    side = lax.axis_index("narrow")
    levels = wide.bit_length() - 1
    enc_rows = enc_ref.shape[0]
    features = cross_ref.shape[1]
    heads_dev = features // HEAD
    chunk_cols = features // chunks
    cap = cross_ref.shape[0] // wide

    place = 0
    for bit in range(levels):
        place = place + ((me // 2**bit) % 2) * 2 ** (levels - 1 - bit)

    def rows_of(device):
        return pl.ds(pl.multiple_of(device * cap, cap), cap)

    def enc_copy(level):
        reach = 2 ** (levels - 1 - level)
        bit = (me // reach) % 2
        start = (place // 2**level) * 2**level
        block = pl.ds(pl.multiple_of(start * enc_rows, enc_rows), 2**level * enc_rows)
        return pltpu.make_async_remote_copy(
            src_ref=enc_buf.at[block],
            dst_ref=enc_buf.at[block],
            send_sem=enc_send.at[level],
            recv_sem=enc_recv.at[level],
            device_id={"wide": me + reach * (1 - 2 * bit)},
            device_id_type=MESH_ID,
        )

    def row_copy(src, dst, send, recv, step):
        peer = lax.rem(me + step, wide)
        return pltpu.make_async_remote_copy(
            src_ref=src.at[rows_of(peer)],
            dst_ref=dst.at[rows_of(me)],
            send_sem=send.at[step],
            recv_sem=recv.at[step],
            device_id={"wide": peer},
            device_id_type=MESH_ID,
        )

    def self_copy(step):
        return row_copy(self_ref, self_raw.at[side], self_send, self_recv, step)

    def kv_copy(step):
        return row_copy(kv_ref, kv_raw, kv_send, kv_recv, step)

    def cross_copy(step, chunk):
        peer = lax.rem(me + step, wide)
        cols = pl.ds(chunk * chunk_cols, chunk_cols)
        return pltpu.make_async_remote_copy(
            src_ref=cross_ref.at[rows_of(peer), cols],
            dst_ref=cross_raw.at[rows_of(me), cols],
            send_sem=cross_send.at[chunk, step],
            recv_sem=cross_recv.at[chunk, step],
            device_id={"wide": peer},
            device_id_type=MESH_ID,
        )

    def side_copy(step, hop):
        rows = rows_of(lax.rem(me - step + wide, wide))
        return pltpu.make_async_remote_copy(
            src_ref=self_raw.at[side, rows],
            dst_ref=self_raw.at[side, rows],
            send_sem=side_send.at[hop - 1, step],
            recv_sem=side_recv.at[hop - 1, step],
            device_id={"narrow": lax.rem(side + hop, narrow)},
            device_id_type=MESH_ID,
        )

    own_block = rows_of(me)
    locals_ = [
        pltpu.make_async_copy(
            enc_ref,
            enc_buf.at[pl.ds(pl.multiple_of(place * enc_rows, enc_rows), enc_rows)],
            local_sem.at[0],
        ),
        pltpu.make_async_copy(
            self_ref.at[own_block], self_raw.at[side, own_block], local_sem.at[1]
        ),
        pltpu.make_async_copy(kv_ref.at[own_block], kv_raw.at[own_block], local_sem.at[2]),
        pltpu.make_async_copy(cross_ref.at[own_block], cross_raw.at[own_block], local_sem.at[3]),
        pltpu.make_async_copy(cache_ref, cache, local_sem.at[4]),
    ]
    for copy in locals_:
        copy.start()
    greet(wide, narrow)
    locals_[0].wait()
    enc_copy(0).start()

    @pl.loop(1, wide)
    def _(step):
        kv_copy(step).start()

    bounds = [1 + (wide - 1) * level // levels for level in range(levels + 1)]
    for level in range(levels):

        @pl.loop(bounds[level], bounds[level + 1])
        def _(step):
            self_copy(step).start()

        enc_copy(level).wait()
        if level + 1 < levels:
            enc_copy(level + 1).start()

    locals_[1].wait()
    for hop in range(1, narrow):
        side_copy(0, hop).start()

    @pl.loop(1, wide)
    def _(step):
        self_copy(step).wait_recv()
        for hop in range(1, narrow):
            side_copy(step, hop).start()
        for chunk in range(chunks):
            cross_copy(step, chunk).start()

    problem = problem_ref[0]
    problem_bits = problems.bit_length() - 1
    for block in range(wide // problems):
        mine = None
        for other in range(problems):
            turned = sum((other >> bit) % 2 << (problem_bits - 1 - bit) for bit in range(problem_bits))
            start = (block * problems + turned) * enc_rows
            rows = enc_buf[start : start + enc_rows, :]
            mine = rows if mine is None else jnp.where(problem == other, rows, mine)
        keys[block * enc_rows : (block + 1) * enc_rows, :] = mine

    locals_[2].wait()

    @pl.loop(1, wide)
    def _(step):
        kv_copy(step).wait()

    fresh[...] = jnp.dot(perm_self_ref[...], kv_raw[...], preferred_element_type=jnp.float32)

    @pl.loop(0, wide)
    def _(step):
        for hop in range(1, narrow):
            side_copy(step, hop).wait()

    total_rows = steps * own
    for part in range(narrow):

        @pl.loop(0, heads_dev)
        def _(head):
            cols = pl.ds(pl.multiple_of(head * HEAD, HEAD), HEAD)
            moved = jnp.dot(
                perm_self_ref[...], self_raw[part, :, cols], preferred_element_type=jnp.float32
            )
            start = pl.multiple_of((part * heads_dev + head) * total_rows, total_rows)
            q_rows[pl.ds(start, total_rows), :] = moved

    locals_[4].wait()

    @pl.loop(0, own, unroll=2)
    def _(cand):
        rows = [
            q_rows[pl.ds(step * own + cand, HEADS, stride=total_rows), :] for step in range(steps)
        ]
        query = jnp.concatenate(rows, axis=0)
        scores = lax.dot_general(
            query.astype(jnp.bfloat16),
            cache[cand, :, :HEAD],
            DOT_T,
            preferred_element_type=jnp.float32,
        )
        row_step = lax.broadcasted_iota(jnp.int32, (steps * HEADS, 1), 0) // HEADS
        peak = jnp.max(scores, axis=1, keepdims=True)
        new = []
        for step in range(steps):
            row = fresh[pl.ds(step * own + cand, 1), :]
            score = jnp.sum(query * row[:, :HEAD], axis=1, keepdims=True)
            score = jnp.where(row_step >= step, score, -jnp.inf)
            peak = jnp.maximum(peak, score)
            new.append((row, score))
        expo = jnp.exp2((scores - peak) * SCALE)
        total = jnp.sum(expo, axis=1, keepdims=True)
        result = jnp.dot(
            expo.astype(jnp.bfloat16), cache[cand, :, HEAD:], preferred_element_type=jnp.float32
        )
        for row, score in new:
            weight = jnp.exp2((score - peak) * SCALE)
            total = total + weight
            result = result + weight.astype(jnp.bfloat16).astype(jnp.float32) * row[:, HEAD:]
        result = result / total
        for step in range(steps):
            o_rows[pl.ds(step * own + cand, HEADS, stride=total_rows), :] = result[
                step * HEADS : (step + 1) * HEADS
            ]

    @pl.loop(0, HEADS)
    def _(head):
        start = pl.multiple_of(head * total_rows, total_rows)
        cols = pl.ds(pl.multiple_of(head * HEAD, HEAD), HEAD)
        self_out[:, cols] = o_rows[pl.ds(start, total_rows), :].astype(jnp.bfloat16)

    locals_[3].wait()
    query_rows = perm_cross_ref.shape[0]
    group = math.gcd(heads_dev // chunks, 4)
    for chunk in range(chunks):

        @pl.loop(1, wide)
        def _(step):
            cross_copy(step, chunk).wait_recv()

        @pl.loop(0, heads_dev // chunks // group)
        def _(index):
            start = pl.multiple_of(chunk * chunk_cols + index * group * HEAD, HEAD)
            cols = pl.ds(start, group * HEAD)
            moved = jnp.dot(
                perm_cross_ref[...], cross_raw[:, cols], preferred_element_type=jnp.float32
            ).astype(jnp.bfloat16)
            query = jnp.concatenate(
                [moved[:, head * HEAD : (head + 1) * HEAD] for head in range(group)], axis=0
            )
            scores = lax.dot_general(
                query, keys[:, :HEAD], DOT_T, preferred_element_type=jnp.float32
            )
            peak = jnp.max(scores, axis=1, keepdims=True)
            expo = jnp.exp2((scores - peak) * SCALE)
            total = jnp.sum(expo, axis=1, keepdims=True)
            result = jnp.dot(
                expo.astype(jnp.bfloat16), keys[:, HEAD:], preferred_element_type=jnp.float32
            )
            result = (result / total).astype(jnp.bfloat16)
            cross_out[:, cols] = jnp.concatenate(
                [result[head * query_rows : (head + 1) * query_rows] for head in range(group)],
                axis=1,
            )

    @pl.loop(1, wide)
    def _(step):
        self_copy(step).wait_send()
        for chunk in range(chunks):
            cross_copy(step, chunk).wait_send()


def attend(problem, enc, cross_rows, self_rows, kv_rows, cache, perm_cross, perm_self, dims):
    wide, narrow, steps, own, problems, chunks = dims
    slots, features = cross_rows.shape
    enc_rows, kv_cols = enc.shape
    levels = wide.bit_length() - 1
    vmem = pl.BlockSpec(memory_space=pltpu.VMEM)
    anywhere = pl.BlockSpec(memory_space=pl.ANY)
    total_rows = steps * own
    bf16 = jnp.bfloat16
    dma = pltpu.SemaphoreType.DMA
    return pl.pallas_call(
        functools.partial(main_kernel, dims),
        out_shape=(
            jax.ShapeDtypeStruct((perm_cross.shape[0], features), bf16),
            jax.ShapeDtypeStruct((total_rows, HEADS * HEAD), bf16),
        ),
        in_specs=[
            pl.BlockSpec(memory_space=pltpu.SMEM),
            anywhere,
            anywhere,
            anywhere,
            anywhere,
            anywhere,
            vmem,
            vmem,
        ],
        out_specs=(vmem, vmem),
        scratch_shapes=[
            pltpu.VMEM((wide * enc_rows, kv_cols), bf16),
            pltpu.VMEM((wide // problems * enc_rows, kv_cols), bf16),
            pltpu.VMEM((slots, features), bf16),
            pltpu.VMEM((narrow, slots, features), bf16),
            pltpu.VMEM((slots, kv_cols), bf16),
            pltpu.VMEM(cache.shape, bf16),
            pltpu.VMEM((total_rows, kv_cols), jnp.float32),
            pltpu.VMEM((HEADS * total_rows, HEAD), jnp.float32),
            pltpu.VMEM((HEADS * total_rows, HEAD), jnp.float32),
            dma((5,)),
            dma((levels,)),
            dma((levels,)),
            dma((wide,)),
            dma((wide,)),
            dma((wide,)),
            dma((wide,)),
            dma((chunks, wide)),
            dma((chunks, wide)),
            dma((narrow - 1, wide)),
            dma((narrow - 1, wide)),
        ],
        compiler_params=pltpu.CompilerParams(
            collective_id=1, has_side_effects=True, vmem_limit_bytes=56 * 2**20
        ),
    )(problem, enc, cross_rows, self_rows, kv_rows, cache, perm_cross, perm_self)


def body(
    enc_hidden,
    enc_gain,
    cross_weight,
    assign,
    token_ids,
    cross_table,
    self_table,
    kv_table,
    self_cache,
):
    wide = lax.axis_size("wide")
    narrow = lax.axis_size("narrow")
    me = lax.axis_index("wide")
    side = lax.axis_index("narrow")
    hidden = enc_hidden.astype(jnp.float32)
    squares = jnp.sum(hidden * hidden, axis=1, keepdims=True)
    scaled = (hidden * enc_gain).astype(jnp.bfloat16)
    proj = jnp.dot(scaled, cross_weight, preferred_element_type=jnp.float32)
    part = jnp.concatenate([proj, jnp.broadcast_to(squares, (proj.shape[0], 128))], axis=1)

    steps, cand = token_ids.shape[1:]
    rows = steps * cand
    own = cand // narrow
    flat = token_ids.reshape(1, rows)
    all_ids, parts = exchange(jnp.broadcast_to(flat, (8, rows)), part, wide, narrow)
    summed = part + jnp.sum(parts, axis=0)
    enc = summed[:, : 2 * HEAD] * lax.rsqrt(summed[:, 2 * HEAD :][:, :1] / D + EPS)
    enc = enc.astype(jnp.bfloat16)

    per_owner = cross_table.shape[0]
    capacity = max(TILE_ROWS, 2 * rows // wide)
    slot = jnp.arange(capacity, dtype=jnp.int32)
    local = all_ids[:, 0, :] - me * per_owner
    mine = (local >= 0) & (local < per_owner)
    count = mine.astype(jnp.int32)
    rank = jnp.cumsum(count, axis=1) - count
    match = mine[:, None, :] & (rank[:, None, :] == slot[None, :, None])
    request = jnp.max(jnp.where(match, local[:, None, :], -1), axis=2).reshape(-1)
    picked = (request[:, None] == jnp.arange(per_owner, dtype=jnp.int32)[None, :]).astype(
        jnp.bfloat16
    )

    def lookup(table):
        return jnp.dot(picked, table, preferred_element_type=jnp.float32).astype(jnp.bfloat16)

    owner = flat[0] // per_owner
    hits = (owner[:, None] == jnp.arange(wide, dtype=jnp.int32)[None, :]).astype(jnp.int32)
    earlier = jnp.cumsum(hits, axis=0) - hits
    target = owner * capacity + jnp.sum(earlier * hits, axis=1)
    perm = (
        target[:, None] == jnp.arange(wide * capacity, dtype=jnp.int32)[None, :]
    ).astype(jnp.bfloat16)
    perm_self = lax.dynamic_slice_in_dim(
        perm.reshape(steps, cand, wide * capacity), side * own, own, 1
    ).reshape(steps * own, wide * capacity)

    problems = wide * enc_hidden.shape[0] // ENC_LEN
    chunks = 2
    dims = (wide, narrow, steps, own, problems, chunks)
    cross, selfs = attend(
        assign,
        enc,
        lookup(cross_table),
        lookup(self_table),
        lookup(kv_table),
        self_cache[0],
        perm,
        perm_self,
        dims,
    )
    return (
        cross.reshape(1, steps, cand, cross.shape[1]),
        selfs.reshape(1, steps, own, HEADS * HEAD),
    )


def solution(mesh):
    placed = (
        P("wide", "narrow"),
        P("narrow"),
        P("narrow", None),
        P("wide"),
        P("wide", None, None),
        P("wide", "narrow"),
        P("wide", "narrow"),
        P("wide", None),
        P("wide", "narrow", None, None),
    )
    return jax.shard_map(
        body,
        mesh=mesh,
        in_specs=placed,
        out_specs=(P("wide", None, None, "narrow"), P("wide", None, "narrow", None)),
        check_vma=False,
    )
```

```python
import functools
import math

import jax
import jax.numpy as jnp
from jax import lax
from jax.experimental import pallas as pl
from jax.experimental.pallas import tpu as pltpu
from jax.sharding import PartitionSpec as P

D = 6144
HEADS = 48
HEAD = 128
ENC_LEN = 1536
EPS = 1e-06
TILE_ROWS = 16
SCALE = HEAD ** (-0.5) * math.log2(math.e)

MESH_ID = pl.DeviceIdType.MESH
DOT_T = (((1,), (1,)), ((), ()))


def most_parts(count, limit=4):
    return max(parts for parts in range(1, limit + 1) if count % parts == 0)


def greet(wide, narrow):
    me = lax.axis_index("wide")
    side = lax.axis_index("narrow")
    barrier = pltpu.get_barrier_semaphore()

    @pl.loop(1, wide)
    def _(step):
        pl.semaphore_signal(
            barrier, inc=1, device_id={"wide": lax.rem(me + step, wide)}, device_id_type=MESH_ID
        )

    for step in range(1, narrow):
        pl.semaphore_signal(
            barrier,
            inc=1,
            device_id={"narrow": lax.rem(side + step, narrow)},
            device_id_type=MESH_ID,
        )
    pl.semaphore_wait(barrier, wide + narrow - 2)


def pick_kernel(wide, per_owner, capacity, ids_ref, picked_out, all_ids, id_send, id_recv):
    me = lax.axis_index("wide")
    greet(wide, 1)

    def ids_copy(step):
        return pltpu.make_async_remote_copy(
            src_ref=ids_ref,
            dst_ref=all_ids.at[me],
            send_sem=id_send.at[step],
            recv_sem=id_recv.at[step],
            device_id={"wide": lax.rem(me + step, wide)},
            device_id_type=MESH_ID,
        )

    @pl.loop(1, wide)
    def _(step):
        ids_copy(step).start()

    all_ids[me] = ids_ref[...]
    rows = ids_ref.shape[1]
    before = lax.broadcasted_iota(jnp.int32, (rows, rows), 0)
    after = lax.broadcasted_iota(jnp.int32, (rows, rows), 1)
    earlier = jnp.where(before < after, 1.0, 0.0).astype(jnp.bfloat16)
    slot = lax.broadcasted_iota(jnp.int32, (capacity, rows), 0).astype(jnp.float32)
    entry = lax.broadcasted_iota(jnp.int32, (capacity, per_owner), 1).astype(jnp.float32)

    @pl.loop(1, wide)
    def _(step):
        ids_copy(step).wait()

    for group in range(wide):
        local = all_ids[group] - me * per_owner
        mine = jnp.where((local >= 0) & (local < per_owner), 1.0, 0.0)
        rank = jnp.dot(mine.astype(jnp.bfloat16), earlier, preferred_element_type=jnp.float32)
        key = jnp.where(mine > 0.0, rank, -1.0)[:1]
        request = jnp.max(
            jnp.where(slot == key, local[:1].astype(jnp.float32), -1.0), axis=1, keepdims=True
        )
        picked_out[group * capacity : (group + 1) * capacity, :] = jnp.where(
            entry == request, 1.0, 0.0
        ).astype(jnp.bfloat16)


def pick(ids, per_owner, capacity, wide):
    vmem = pl.BlockSpec(memory_space=pltpu.VMEM)
    return pl.pallas_call(
        functools.partial(pick_kernel, wide, per_owner, capacity),
        out_shape=jax.ShapeDtypeStruct((wide * capacity, per_owner), jnp.bfloat16),
        in_specs=[vmem],
        out_specs=vmem,
        scratch_shapes=[
            pltpu.VMEM((wide,) + ids.shape, ids.dtype),
            pltpu.SemaphoreType.DMA((wide,)),
            pltpu.SemaphoreType.DMA((wide,)),
        ],
        compiler_params=pltpu.CompilerParams(collective_id=0, has_side_effects=True),
    )(ids)


def main_kernel(
    dims,
    problem_ref,
    ids_ref,
    hidden_ref,
    gain_ref,
    weight_ref,
    picked_ref,
    table_ref,
    self_ref,
    kv_ref,
    cache_ref,
    cross_out,
    self_out,
    hidden,
    weight,
    table,
    part,
    parts,
    cross_ref,
    perm_cross_ref,
    perm_self_ref,
    enc_buf,
    keys,
    cross_raw,
    self_raw,
    kv_raw,
    cache,
    fresh,
    q_rows,
    o_rows,
    local_sem,
    part_send,
    part_recv,
    enc_send,
    enc_recv,
    self_send,
    self_recv,
    kv_send,
    kv_recv,
    cross_send,
    cross_recv,
    side_send,
    side_recv,
):
    wide, narrow, steps, own, problems, chunks = dims
    me = lax.axis_index("wide")
    side = lax.axis_index("narrow")
    levels = wide.bit_length() - 1
    enc_rows = hidden_ref.shape[0]
    features = cross_ref.shape[1]
    kv_cols = kv_ref.shape[1]
    heads_dev = features // HEAD
    chunk_cols = features // chunks
    cap = cross_ref.shape[0] // wide

    place = 0
    for bit in range(levels):
        place = place + ((me // 2**bit) % 2) * 2 ** (levels - 1 - bit)

    def rows_of(device):
        return pl.ds(pl.multiple_of(device * cap, cap), cap)

    def enc_copy(level):
        reach = 2 ** (levels - 1 - level)
        bit = (me // reach) % 2
        start = (place // 2**level) * 2**level
        block = pl.ds(pl.multiple_of(start * enc_rows, enc_rows), 2**level * enc_rows)
        return pltpu.make_async_remote_copy(
            src_ref=enc_buf.at[block],
            dst_ref=enc_buf.at[block],
            send_sem=enc_send.at[level],
            recv_sem=enc_recv.at[level],
            device_id={"wide": me + reach * (1 - 2 * bit)},
            device_id_type=MESH_ID,
        )

    def row_copy(src, dst, send, recv, step):
        peer = lax.rem(me + step, wide)
        return pltpu.make_async_remote_copy(
            src_ref=src.at[rows_of(peer)],
            dst_ref=dst.at[rows_of(me)],
            send_sem=send.at[step],
            recv_sem=recv.at[step],
            device_id={"wide": peer},
            device_id_type=MESH_ID,
        )

    def self_copy(step):
        return row_copy(self_ref, self_raw.at[side], self_send, self_recv, step)

    def kv_copy(step):
        return row_copy(kv_ref, kv_raw, kv_send, kv_recv, step)

    def cross_copy(step, chunk):
        peer = lax.rem(me + step, wide)
        cols = pl.ds(chunk * chunk_cols, chunk_cols)
        return pltpu.make_async_remote_copy(
            src_ref=cross_ref.at[rows_of(peer), cols],
            dst_ref=cross_raw.at[rows_of(me), cols],
            send_sem=cross_send.at[chunk, step],
            recv_sem=cross_recv.at[chunk, step],
            device_id={"wide": peer},
            device_id_type=MESH_ID,
        )

    def side_copy(step, hop):
        rows = rows_of(lax.rem(me - step + wide, wide))
        return pltpu.make_async_remote_copy(
            src_ref=self_raw.at[side, rows],
            dst_ref=self_raw.at[side, rows],
            send_sem=side_send.at[hop - 1, step],
            recv_sem=side_recv.at[hop - 1, step],
            device_id={"narrow": lax.rem(side + hop, narrow)},
            device_id_type=MESH_ID,
        )

    def part_copy(hop):
        return pltpu.make_async_remote_copy(
            src_ref=part,
            dst_ref=parts.at[hop - 1],
            send_sem=part_send.at[hop - 1],
            recv_sem=part_recv.at[hop - 1],
            device_id={"narrow": lax.rem(side + hop, narrow)},
            device_id_type=MESH_ID,
        )

    own_block = rows_of(me)
    locals_ = [
        pltpu.make_async_copy(hidden_ref, hidden, local_sem.at[0]),
        pltpu.make_async_copy(
            self_ref.at[own_block], self_raw.at[side, own_block], local_sem.at[1]
        ),
        pltpu.make_async_copy(kv_ref.at[own_block], kv_raw.at[own_block], local_sem.at[2]),
        pltpu.make_async_copy(weight_ref, weight, local_sem.at[3]),
        pltpu.make_async_copy(table_ref, table, local_sem.at[4]),
        pltpu.make_async_copy(cache_ref, cache, local_sem.at[5]),
    ]
    for copy in locals_:
        copy.start()
    greet(wide, narrow)

    @pl.loop(1, wide)
    def _(step):
        kv_copy(step).start()
        self_copy(step).start()

    locals_[1].wait()
    for hop in range(1, narrow):
        side_copy(0, hop).start()

    locals_[0].wait()
    locals_[3].wait()
    part[...] = jnp.zeros_like(part)
    depth = 256

    @pl.loop(0, hidden.shape[1] // depth)
    def _(index):
        span = pl.ds(pl.multiple_of(index * depth, depth), depth)
        values = hidden[:, span].astype(jnp.float32)
        scaled = (values * gain_ref[:, span]).astype(jnp.bfloat16)
        part[:, :kv_cols] += jnp.dot(scaled, weight[span, :], preferred_element_type=jnp.float32)
        squares = values * values
        part[:, kv_cols:] += sum(
            squares[:, lane : lane + HEAD] for lane in range(0, depth, HEAD)
        )

    locals_[4].wait()

    @pl.loop(0, features // 256)
    def _(index):
        cols = pl.ds(pl.multiple_of(index * 256, 256), 256)
        cross_ref[:, cols] = jnp.dot(
            picked_ref[...], table[:, cols], preferred_element_type=jnp.float32
        ).astype(jnp.bfloat16)

    for hop in range(1, narrow):
        part_copy(hop).start()

    rows_total = ids_ref.shape[1]
    per_owner = table_ref.shape[0]
    ids = ids_ref[:1, :]
    owner = jnp.zeros_like(ids)
    for device in range(1, wide):
        owner = owner + jnp.where(ids >= device * per_owner, 1, 0)
    across = jnp.broadcast_to(owner.astype(jnp.float32), (rows_total, rows_total))
    down = jnp.transpose(across)
    row = lax.broadcasted_iota(jnp.int32, (rows_total, rows_total), 0)
    col = lax.broadcasted_iota(jnp.int32, (rows_total, rows_total), 1)
    rank = jnp.sum(jnp.where((across == down) & (col < row), 1.0, 0.0), axis=1, keepdims=True)
    target = down[:, :1] * cap + rank
    place_of = lax.broadcasted_iota(jnp.int32, perm_cross_ref.shape, 1).astype(jnp.float32)
    perm_cross_ref[...] = jnp.where(place_of == target, 1.0, 0.0).astype(jnp.bfloat16)
    cand = rows_total // steps
    for step in range(steps):
        mine = pl.ds(pl.multiple_of(step * cand + side * own, own), own)
        perm_self_ref[step * own : (step + 1) * own, :] = perm_cross_ref[mine, :]

    def pass_on(step):
        self_copy(step).wait_recv()
        for hop in range(1, narrow):
            side_copy(step, hop).start()
        cross_copy(step, 0).start()

    early = 1 + (wide - 1) // 4
    pl.loop(1, early)(pass_on)

    for hop in range(1, narrow):
        part_copy(hop).wait()
    summed = part[...]
    for hop in range(1, narrow):
        summed = summed + parts[hop - 1]
    squares = jnp.sum(summed[:, kv_cols:], axis=1, keepdims=True)
    enc_buf[pl.ds(pl.multiple_of(place * enc_rows, enc_rows), enc_rows), :] = (
        summed[:, :kv_cols] * lax.rsqrt(squares / D + EPS)
    ).astype(jnp.bfloat16)

    pl.loop(early, early + 1)(pass_on)
    enc_copy(0).start()
    pl.loop(early + 1, wide)(pass_on)
    cross_raw[own_block, :] = cross_ref[own_block, :]

    for level in range(levels - 2):
        enc_copy(level).wait()
        enc_copy(level + 1).start()
    for chunk in range(1, chunks):

        @pl.loop(1, wide)
        def _(step):
            cross_copy(step, chunk).start()

    locals_[2].wait()

    @pl.loop(1, wide)
    def _(step):
        kv_copy(step).wait()

    fresh[...] = jnp.dot(perm_self_ref[...], kv_raw[...], preferred_element_type=jnp.float32)

    @pl.loop(0, wide)
    def _(step):
        for hop in range(1, narrow):
            side_copy(step, hop).wait()

    total_rows = steps * own
    for other in range(narrow):

        @pl.loop(0, heads_dev)
        def _(head):
            cols = pl.ds(pl.multiple_of(head * HEAD, HEAD), HEAD)
            moved = jnp.dot(
                perm_self_ref[...], self_raw[other, :, cols], preferred_element_type=jnp.float32
            )
            start = pl.multiple_of((other * heads_dev + head) * total_rows, total_rows)
            q_rows[pl.ds(start, total_rows), :] = moved

    locals_[5].wait()

    def attend_one(cand):
        rows = [
            q_rows[pl.ds(step * own + cand, HEADS, stride=total_rows), :] for step in range(steps)
        ]
        query = jnp.concatenate(rows, axis=0)
        scores = lax.dot_general(
            query.astype(jnp.bfloat16),
            cache[cand, :, :HEAD],
            DOT_T,
            preferred_element_type=jnp.float32,
        )
        row_step = lax.broadcasted_iota(jnp.int32, (steps * HEADS, 1), 0) // HEADS
        peak = jnp.max(scores, axis=1, keepdims=True)
        new = []
        for step in range(steps):
            row = fresh[pl.ds(step * own + cand, 1), :]
            score = jnp.sum(query * row[:, :HEAD], axis=1, keepdims=True)
            score = jnp.where(row_step >= step, score, -jnp.inf)
            peak = jnp.maximum(peak, score)
            new.append((row, score))
        expo = jnp.exp2((scores - peak) * SCALE)
        total = jnp.sum(expo, axis=1, keepdims=True)
        result = jnp.dot(
            expo.astype(jnp.bfloat16), cache[cand, :, HEAD:], preferred_element_type=jnp.float32
        )
        for row, score in new:
            weight = jnp.exp2((score - peak) * SCALE)
            total = total + weight
            result = result + weight.astype(jnp.bfloat16).astype(jnp.float32) * row[:, HEAD:]
        result = result / total
        for step in range(steps):
            o_rows[pl.ds(step * own + cand, HEADS, stride=total_rows), :] = result[
                step * HEADS : (step + 1) * HEADS
            ]

    enc_copy(levels - 2).wait()
    enc_copy(levels - 1).start()
    pl.loop(0, own, unroll=2)(attend_one)
    enc_copy(levels - 1).wait()

    @pl.loop(0, HEADS)
    def _(head):
        start = pl.multiple_of(head * total_rows, total_rows)
        cols = pl.ds(pl.multiple_of(head * HEAD, HEAD), HEAD)
        self_out[:, cols] = o_rows[pl.ds(start, total_rows), :].astype(jnp.bfloat16)

    problem = problem_ref[0]
    problem_bits = problems.bit_length() - 1
    for block in range(wide // problems):
        mine = None
        for other in range(problems):
            turned = sum((other >> bit) % 2 << (problem_bits - 1 - bit) for bit in range(problem_bits))
            start = (block * problems + turned) * enc_rows
            rows = enc_buf[start : start + enc_rows, :]
            mine = rows if mine is None else jnp.where(problem == other, rows, mine)
        keys[block * enc_rows : (block + 1) * enc_rows, :] = mine

    query_rows = perm_cross_ref.shape[0]
    group = most_parts(heads_dev // chunks)
    for chunk in range(chunks):

        @pl.loop(1, wide)
        def _(step):
            cross_copy(step, chunk).wait_recv()

        @pl.loop(0, heads_dev // chunks // group)
        def _(index):
            start = pl.multiple_of(chunk * chunk_cols + index * group * HEAD, HEAD)
            cols = pl.ds(start, group * HEAD)
            moved = jnp.dot(
                perm_cross_ref[...], cross_raw[:, cols], preferred_element_type=jnp.float32
            ).astype(jnp.bfloat16)
            query = jnp.concatenate(
                [moved[:, head * HEAD : (head + 1) * HEAD] for head in range(group)], axis=0
            )
            scores = lax.dot_general(
                query, keys[:, :HEAD], DOT_T, preferred_element_type=jnp.float32
            )
            peak = jnp.max(scores, axis=1, keepdims=True)
            expo = jnp.exp2((scores - peak) * SCALE)
            total = jnp.sum(expo, axis=1, keepdims=True)
            result = jnp.dot(
                expo.astype(jnp.bfloat16), keys[:, HEAD:], preferred_element_type=jnp.float32
            )
            result = (result / total).astype(jnp.bfloat16)
            cross_out[:, cols] = jnp.concatenate(
                [result[head * query_rows : (head + 1) * query_rows] for head in range(group)],
                axis=1,
            )

    @pl.loop(1, wide)
    def _(step):
        self_copy(step).wait_send()
        for chunk in range(chunks):
            cross_copy(step, chunk).wait_send()


def attend(problem, ids, hidden, gain, weight, picked, table, self_rows, kv_rows, cache, dims):
    wide, narrow, steps, own, problems, chunks = dims
    slots, features = self_rows.shape
    enc_rows = hidden.shape[0]
    kv_cols = kv_rows.shape[1]
    levels = wide.bit_length() - 1
    vmem = pl.BlockSpec(memory_space=pltpu.VMEM)
    anywhere = pl.BlockSpec(memory_space=pl.ANY)
    total_rows = steps * own
    bf16 = jnp.bfloat16
    dma = pltpu.SemaphoreType.DMA
    part = (enc_rows, kv_cols + HEAD)
    return pl.pallas_call(
        functools.partial(main_kernel, dims),
        out_shape=(
            jax.ShapeDtypeStruct((ids.shape[1], features), bf16),
            jax.ShapeDtypeStruct((total_rows, HEADS * HEAD), bf16),
        ),
        in_specs=[
            pl.BlockSpec(memory_space=pltpu.SMEM),
            vmem,
            anywhere,
            vmem,
            anywhere,
            vmem,
            anywhere,
            anywhere,
            anywhere,
            anywhere,
        ],
        out_specs=(vmem, vmem),
        scratch_shapes=[
            pltpu.VMEM(hidden.shape, bf16),
            pltpu.VMEM(weight.shape, bf16),
            pltpu.VMEM(table.shape, bf16),
            pltpu.VMEM(part, jnp.float32),
            pltpu.VMEM((narrow - 1,) + part, jnp.float32),
            pltpu.VMEM((slots, features), bf16),
            pltpu.VMEM((ids.shape[1], slots), bf16),
            pltpu.VMEM((total_rows, slots), bf16),
            pltpu.VMEM((wide * enc_rows, kv_cols), bf16),
            pltpu.VMEM((wide // problems * enc_rows, kv_cols), bf16),
            pltpu.VMEM((slots, features), bf16),
            pltpu.VMEM((narrow, slots, features), bf16),
            pltpu.VMEM((slots, kv_cols), bf16),
            pltpu.VMEM(cache.shape, bf16),
            pltpu.VMEM((total_rows, kv_cols), jnp.float32),
            pltpu.VMEM((HEADS * total_rows, HEAD), jnp.float32),
            pltpu.VMEM((HEADS * total_rows, HEAD), jnp.float32),
            dma((6,)),
            dma((narrow - 1,)),
            dma((narrow - 1,)),
            dma((levels,)),
            dma((levels,)),
            dma((wide,)),
            dma((wide,)),
            dma((wide,)),
            dma((wide,)),
            dma((chunks, wide)),
            dma((chunks, wide)),
            dma((narrow - 1, wide)),
            dma((narrow - 1, wide)),
        ],
        compiler_params=pltpu.CompilerParams(
            collective_id=1, has_side_effects=True, vmem_limit_bytes=56 * 2**20
        ),
    )(problem, ids, hidden, gain, weight, picked, table, self_rows, kv_rows, cache)


def body(
    enc_hidden,
    enc_gain,
    cross_weight,
    assign,
    token_ids,
    cross_table,
    self_table,
    kv_table,
    self_cache,
):
    wide = lax.axis_size("wide")
    narrow = lax.axis_size("narrow")
    steps, cand = token_ids.shape[1:]
    rows = steps * cand
    own = cand // narrow
    per_owner = cross_table.shape[0]
    capacity = max(TILE_ROWS, 2 * rows // wide)
    ids = jnp.broadcast_to(token_ids.reshape(1, rows), (8, rows))
    picked = pick(ids, per_owner, capacity, wide)

    def lookup(table):
        return jnp.dot(picked, table, preferred_element_type=jnp.float32).astype(jnp.bfloat16)

    problems = wide * enc_hidden.shape[0] // ENC_LEN
    chunks = most_parts(cross_table.shape[1] // HEAD)
    cross, selfs = attend(
        assign,
        ids,
        enc_hidden,
        enc_gain.reshape(1, -1),
        cross_weight,
        picked,
        cross_table,
        lookup(self_table),
        lookup(kv_table),
        self_cache[0],
        (wide, narrow, steps, own, problems, chunks),
    )
    return (
        cross.reshape(1, steps, cand, cross.shape[1]),
        selfs.reshape(1, steps, own, HEADS * HEAD),
    )


def solution(mesh):
    placed = (
        P("wide", "narrow"),
        P("narrow"),
        P("narrow", None),
        P("wide"),
        P("wide", None, None),
        P("wide", "narrow"),
        P("wide", "narrow"),
        P("wide", None),
        P("wide", "narrow", None, None),
    )
    return jax.shard_map(
        body,
        mesh=mesh,
        in_specs=placed,
        out_specs=(P("wide", None, None, "narrow"), P("wide", None, "narrow", None)),
        check_vma=False,
    )
```

```python
import functools
import math

import jax
import jax.numpy as jnp
from jax import lax
from jax.experimental import pallas as pl
from jax.experimental.pallas import tpu as pltpu
from jax.sharding import PartitionSpec as P

D = 6144
HEADS = 48
HEAD = 128
ENC_LEN = 1536
EPS = 1e-06
TILE_ROWS = 16
SCALE = HEAD ** (-0.5) * math.log2(math.e)

MESH_ID = pl.DeviceIdType.MESH
DOT_T = (((1,), (1,)), ((), ()))


def most_parts(count, limit=4):
    return max(parts for parts in range(1, limit + 1) if count % parts == 0)


def greet(wide, narrow):
    me = lax.axis_index("wide")
    side = lax.axis_index("narrow")
    barrier = pltpu.get_barrier_semaphore()

    @pl.loop(1, wide)
    def _(step):
        pl.semaphore_signal(
            barrier, inc=1, device_id={"wide": lax.rem(me + step, wide)}, device_id_type=MESH_ID
        )

    for step in range(1, narrow):
        pl.semaphore_signal(
            barrier,
            inc=1,
            device_id={"narrow": lax.rem(side + step, narrow)},
            device_id_type=MESH_ID,
        )
    pl.semaphore_wait(barrier, wide + narrow - 2)


def pick_kernel(wide, per_owner, capacity, ids_ref, picked_out, all_ids, id_send, id_recv):
    me = lax.axis_index("wide")
    greet(wide, 1)

    def ids_copy(step):
        return pltpu.make_async_remote_copy(
            src_ref=ids_ref,
            dst_ref=all_ids.at[me],
            send_sem=id_send.at[step],
            recv_sem=id_recv.at[step],
            device_id={"wide": lax.rem(me + step, wide)},
            device_id_type=MESH_ID,
        )

    @pl.loop(1, wide)
    def _(step):
        ids_copy(step).start()

    all_ids[me] = ids_ref[...]
    rows = ids_ref.shape[1]
    before = lax.broadcasted_iota(jnp.int32, (rows, rows), 0)
    after = lax.broadcasted_iota(jnp.int32, (rows, rows), 1)
    earlier = jnp.where(before < after, 1.0, 0.0).astype(jnp.bfloat16)
    slot = lax.broadcasted_iota(jnp.int32, (capacity, rows), 0).astype(jnp.float32)
    entry = lax.broadcasted_iota(jnp.int32, (capacity, per_owner), 1).astype(jnp.float32)

    @pl.loop(1, wide)
    def _(step):
        ids_copy(step).wait()

    for group in range(wide):
        local = all_ids[group] - me * per_owner
        mine = jnp.where((local >= 0) & (local < per_owner), 1.0, 0.0)
        rank = jnp.dot(mine.astype(jnp.bfloat16), earlier, preferred_element_type=jnp.float32)
        key = jnp.where(mine > 0.0, rank, -1.0)[:1]
        request = jnp.max(
            jnp.where(slot == key, local[:1].astype(jnp.float32), -1.0), axis=1, keepdims=True
        )
        picked_out[group * capacity : (group + 1) * capacity, :] = jnp.where(
            entry == request, 1.0, 0.0
        ).astype(jnp.bfloat16)


def pick(ids, per_owner, capacity, wide):
    vmem = pl.BlockSpec(memory_space=pltpu.VMEM)
    return pl.pallas_call(
        functools.partial(pick_kernel, wide, per_owner, capacity),
        out_shape=jax.ShapeDtypeStruct((wide * capacity, per_owner), jnp.bfloat16),
        in_specs=[vmem],
        out_specs=vmem,
        scratch_shapes=[
            pltpu.VMEM((wide,) + ids.shape, ids.dtype),
            pltpu.SemaphoreType.DMA((wide,)),
            pltpu.SemaphoreType.DMA((wide,)),
        ],
        compiler_params=pltpu.CompilerParams(collective_id=0, has_side_effects=True),
    )(ids)


def main_kernel(
    dims,
    problem_ref,
    ids_ref,
    hidden_ref,
    gain_ref,
    weight_ref,
    picked_ref,
    table_ref,
    self_ref,
    kv_ref,
    cache_ref,
    cross_out,
    self_out,
    hidden,
    weight,
    table,
    part,
    parts,
    cross_ref,
    perm_cross_ref,
    perm_self_ref,
    enc_buf,
    keys,
    cross_raw,
    self_raw,
    kv_raw,
    cache,
    fresh,
    q_rows,
    o_rows,
    local_sem,
    part_send,
    part_recv,
    enc_send,
    enc_recv,
    self_send,
    self_recv,
    kv_send,
    kv_recv,
    cross_send,
    cross_recv,
    side_send,
    side_recv,
):
    wide, narrow, steps, own, problems, chunks = dims
    me = lax.axis_index("wide")
    side = lax.axis_index("narrow")
    levels = wide.bit_length() - 1
    enc_rows = hidden_ref.shape[0]
    features = cross_ref.shape[1]
    kv_cols = kv_ref.shape[1]
    heads_dev = features // HEAD
    chunk_cols = features // chunks
    cap = cross_ref.shape[0] // wide

    place = 0
    for bit in range(levels):
        place = place + ((me // 2**bit) % 2) * 2 ** (levels - 1 - bit)

    def rows_of(device):
        return pl.ds(pl.multiple_of(device * cap, cap), cap)

    def enc_copy(level):
        reach = 2 ** (levels - 1 - level)
        bit = (me // reach) % 2
        start = (place // 2**level) * 2**level
        block = pl.ds(pl.multiple_of(start * enc_rows, enc_rows), 2**level * enc_rows)
        return pltpu.make_async_remote_copy(
            src_ref=enc_buf.at[block],
            dst_ref=enc_buf.at[block],
            send_sem=enc_send.at[level],
            recv_sem=enc_recv.at[level],
            device_id={"wide": me + reach * (1 - 2 * bit)},
            device_id_type=MESH_ID,
        )

    def row_copy(src, dst, send, recv, step):
        peer = lax.rem(me + step, wide)
        return pltpu.make_async_remote_copy(
            src_ref=src.at[rows_of(peer)],
            dst_ref=dst.at[rows_of(me)],
            send_sem=send.at[step],
            recv_sem=recv.at[step],
            device_id={"wide": peer},
            device_id_type=MESH_ID,
        )

    def self_copy(step):
        return row_copy(self_ref, self_raw.at[side], self_send, self_recv, step)

    def kv_copy(step):
        return row_copy(kv_ref, kv_raw, kv_send, kv_recv, step)

    def cross_copy(step, chunk):
        peer = lax.rem(me + step, wide)
        cols = pl.ds(chunk * chunk_cols, chunk_cols)
        return pltpu.make_async_remote_copy(
            src_ref=cross_ref.at[rows_of(peer), cols],
            dst_ref=cross_raw.at[rows_of(me), cols],
            send_sem=cross_send.at[chunk, step],
            recv_sem=cross_recv.at[chunk, step],
            device_id={"wide": peer},
            device_id_type=MESH_ID,
        )

    def side_copy(step, hop):
        rows = rows_of(lax.rem(me - step + wide, wide))
        return pltpu.make_async_remote_copy(
            src_ref=self_raw.at[side, rows],
            dst_ref=self_raw.at[side, rows],
            send_sem=side_send.at[hop - 1, step],
            recv_sem=side_recv.at[hop - 1, step],
            device_id={"narrow": lax.rem(side + hop, narrow)},
            device_id_type=MESH_ID,
        )

    def part_copy(hop):
        return pltpu.make_async_remote_copy(
            src_ref=part,
            dst_ref=parts.at[hop - 1],
            send_sem=part_send.at[hop - 1],
            recv_sem=part_recv.at[hop - 1],
            device_id={"narrow": lax.rem(side + hop, narrow)},
            device_id_type=MESH_ID,
        )

    own_block = rows_of(me)
    locals_ = [
        pltpu.make_async_copy(hidden_ref, hidden, local_sem.at[0]),
        pltpu.make_async_copy(
            self_ref.at[own_block], self_raw.at[side, own_block], local_sem.at[1]
        ),
        pltpu.make_async_copy(kv_ref.at[own_block], kv_raw.at[own_block], local_sem.at[2]),
        pltpu.make_async_copy(weight_ref, weight, local_sem.at[3]),
        pltpu.make_async_copy(table_ref, table, local_sem.at[4]),
        pltpu.make_async_copy(cache_ref, cache, local_sem.at[5]),
    ]
    for copy in locals_:
        copy.start()
    greet(wide, narrow)

    window = min(6, wide - 1)

    def turn(index):
        return lax.rem(index + wide // 2 - 2, wide - 1) + 1

    @pl.loop(1, 1 + window)
    def _(index):
        self_copy(turn(index)).start()

    @pl.loop(1, wide)
    def _(step):
        kv_copy(step).start()

    locals_[1].wait()
    for hop in range(1, narrow):
        side_copy(0, hop).start()

    locals_[0].wait()
    locals_[3].wait()
    part[...] = jnp.zeros_like(part)
    depth = 256

    @pl.loop(0, hidden.shape[1] // depth)
    def _(index):
        span = pl.ds(pl.multiple_of(index * depth, depth), depth)
        values = hidden[:, span].astype(jnp.float32)
        scaled = (values * gain_ref[:, span]).astype(jnp.bfloat16)
        part[:, :kv_cols] += jnp.dot(scaled, weight[span, :], preferred_element_type=jnp.float32)
        squares = values * values
        part[:, kv_cols:] += sum(
            squares[:, lane : lane + HEAD] for lane in range(0, depth, HEAD)
        )

    locals_[4].wait()

    @pl.loop(0, features // 256)
    def _(index):
        cols = pl.ds(pl.multiple_of(index * 256, 256), 256)
        cross_ref[:, cols] = jnp.dot(
            picked_ref[...], table[:, cols], preferred_element_type=jnp.float32
        ).astype(jnp.bfloat16)

    for hop in range(1, narrow):
        part_copy(hop).start()

    rows_total = ids_ref.shape[1]
    per_owner = table_ref.shape[0]
    ids = ids_ref[:1, :]
    owner = jnp.zeros_like(ids)
    for device in range(1, wide):
        owner = owner + jnp.where(ids >= device * per_owner, 1, 0)
    across = jnp.broadcast_to(owner.astype(jnp.float32), (rows_total, rows_total))
    down = jnp.transpose(across)
    row = lax.broadcasted_iota(jnp.int32, (rows_total, rows_total), 0)
    col = lax.broadcasted_iota(jnp.int32, (rows_total, rows_total), 1)
    rank = jnp.sum(jnp.where((across == down) & (col < row), 1.0, 0.0), axis=1, keepdims=True)
    target = down[:, :1] * cap + rank
    place_of = lax.broadcasted_iota(jnp.int32, perm_cross_ref.shape, 1).astype(jnp.float32)
    perm_cross_ref[...] = jnp.where(place_of == target, 1.0, 0.0).astype(jnp.bfloat16)
    cand = rows_total // steps
    for step in range(steps):
        mine = pl.ds(pl.multiple_of(step * cand + side * own, own), own)
        perm_self_ref[step * own : (step + 1) * own, :] = perm_cross_ref[mine, :]

    def pass_on(index):
        step = turn(index)
        self_copy(step).wait_recv()
        for hop in range(1, narrow):
            side_copy(step, hop).start()

    def pass_and_self(index):
        pass_on(index)
        self_copy(turn(index + window)).start()

    def pass_and_cross(index):
        pass_on(index)
        cross_copy(turn(index - (wide - 1 - window)), 0).start()

    def advance(first, last):
        middle = min(max(first, wide - window), last)
        if first < middle:
            pl.loop(first, middle)(pass_and_self)
        if middle < last:
            pl.loop(middle, last)(pass_and_cross)

    marks = [1 + (wide - 1) * k // 15 for k in (4, 5, 9, 13)]
    advance(1, marks[0])

    for hop in range(1, narrow):
        part_copy(hop).wait()
    summed = part[...]
    for hop in range(1, narrow):
        summed = summed + parts[hop - 1]
    squares = jnp.sum(summed[:, kv_cols:], axis=1, keepdims=True)
    enc_buf[pl.ds(pl.multiple_of(place * enc_rows, enc_rows), enc_rows), :] = (
        summed[:, :kv_cols] * lax.rsqrt(squares / D + EPS)
    ).astype(jnp.bfloat16)

    advance(marks[0], marks[1])
    enc_copy(0).start()
    for level in (1, 2):
        advance(marks[level], marks[level + 1])
        if level < levels - 1:
            enc_copy(level - 1).wait()
            enc_copy(level).start()
    advance(marks[3], wide)
    cross_raw[own_block, :] = cross_ref[own_block, :]
    for level in range(3, levels - 1):
        enc_copy(level - 1).wait()
        enc_copy(level).start()

    @pl.loop(1 + window, wide)
    def _(index):
        cross_copy(turn(index), 0).start()

    for chunk in range(1, chunks):

        @pl.loop(1, wide)
        def _(index):
            cross_copy(turn(index), chunk).start()

    locals_[2].wait()

    @pl.loop(1, wide)
    def _(step):
        kv_copy(step).wait()

    fresh[...] = jnp.dot(perm_self_ref[...], kv_raw[...], preferred_element_type=jnp.float32)

    @pl.loop(0, wide)
    def _(step):
        for hop in range(1, narrow):
            side_copy(step, hop).wait()

    total_rows = steps * own
    for other in range(narrow):

        @pl.loop(0, heads_dev)
        def _(head):
            cols = pl.ds(pl.multiple_of(head * HEAD, HEAD), HEAD)
            moved = jnp.dot(
                perm_self_ref[...], self_raw[other, :, cols], preferred_element_type=jnp.float32
            )
            start = pl.multiple_of((other * heads_dev + head) * total_rows, total_rows)
            q_rows[pl.ds(start, total_rows), :] = moved

    locals_[5].wait()

    def attend_one(cand):
        rows = [
            q_rows[pl.ds(step * own + cand, HEADS, stride=total_rows), :] for step in range(steps)
        ]
        query = jnp.concatenate(rows, axis=0)
        scores = lax.dot_general(
            query.astype(jnp.bfloat16),
            cache[cand, :, :HEAD],
            DOT_T,
            preferred_element_type=jnp.float32,
        )
        row_step = lax.broadcasted_iota(jnp.int32, (steps * HEADS, 1), 0) // HEADS
        peak = jnp.max(scores, axis=1, keepdims=True)
        new = []
        for step in range(steps):
            row = fresh[pl.ds(step * own + cand, 1), :]
            score = jnp.sum(query * row[:, :HEAD], axis=1, keepdims=True)
            score = jnp.where(row_step >= step, score, -jnp.inf)
            peak = jnp.maximum(peak, score)
            new.append((row, score))
        expo = jnp.exp2((scores - peak) * SCALE)
        total = jnp.sum(expo, axis=1, keepdims=True)
        result = jnp.dot(
            expo.astype(jnp.bfloat16), cache[cand, :, HEAD:], preferred_element_type=jnp.float32
        )
        for row, score in new:
            weight = jnp.exp2((score - peak) * SCALE)
            total = total + weight
            result = result + weight.astype(jnp.bfloat16).astype(jnp.float32) * row[:, HEAD:]
        result = result / total
        for step in range(steps):
            o_rows[pl.ds(step * own + cand, HEADS, stride=total_rows), :] = result[
                step * HEADS : (step + 1) * HEADS
            ]

    pl.loop(0, own // 2, unroll=2)(attend_one)
    enc_copy(levels - 2).wait()
    enc_copy(levels - 1).start()
    pl.loop(own // 2, own, unroll=2)(attend_one)
    enc_copy(levels - 1).wait()

    @pl.loop(0, HEADS)
    def _(head):
        start = pl.multiple_of(head * total_rows, total_rows)
        cols = pl.ds(pl.multiple_of(head * HEAD, HEAD), HEAD)
        self_out[:, cols] = o_rows[pl.ds(start, total_rows), :].astype(jnp.bfloat16)

    problem = problem_ref[0]
    problem_bits = problems.bit_length() - 1
    for block in range(wide // problems):
        mine = None
        for other in range(problems):
            turned = sum((other >> bit) % 2 << (problem_bits - 1 - bit) for bit in range(problem_bits))
            start = (block * problems + turned) * enc_rows
            rows = enc_buf[start : start + enc_rows, :]
            mine = rows if mine is None else jnp.where(problem == other, rows, mine)
        keys[block * enc_rows : (block + 1) * enc_rows, :] = mine

    query_rows = perm_cross_ref.shape[0]
    group = most_parts(heads_dev // chunks)
    for chunk in range(chunks):

        @pl.loop(1, wide)
        def _(step):
            cross_copy(step, chunk).wait_recv()

        @pl.loop(0, heads_dev // chunks // group)
        def _(index):
            start = pl.multiple_of(chunk * chunk_cols + index * group * HEAD, HEAD)
            cols = pl.ds(start, group * HEAD)
            moved = jnp.dot(
                perm_cross_ref[...], cross_raw[:, cols], preferred_element_type=jnp.float32
            ).astype(jnp.bfloat16)
            query = jnp.concatenate(
                [moved[:, head * HEAD : (head + 1) * HEAD] for head in range(group)], axis=0
            )
            scores = lax.dot_general(
                query, keys[:, :HEAD], DOT_T, preferred_element_type=jnp.float32
            )
            peak = jnp.max(scores, axis=1, keepdims=True)
            expo = jnp.exp2((scores - peak) * SCALE)
            total = jnp.sum(expo, axis=1, keepdims=True)
            result = jnp.dot(
                expo.astype(jnp.bfloat16), keys[:, HEAD:], preferred_element_type=jnp.float32
            )
            result = (result / total).astype(jnp.bfloat16)
            cross_out[:, cols] = jnp.concatenate(
                [result[head * query_rows : (head + 1) * query_rows] for head in range(group)],
                axis=1,
            )

    @pl.loop(1, wide)
    def _(step):
        self_copy(step).wait_send()
        for chunk in range(chunks):
            cross_copy(step, chunk).wait_send()


def attend(problem, ids, hidden, gain, weight, picked, table, self_rows, kv_rows, cache, dims):
    wide, narrow, steps, own, problems, chunks = dims
    slots, features = self_rows.shape
    enc_rows = hidden.shape[0]
    kv_cols = kv_rows.shape[1]
    levels = wide.bit_length() - 1
    vmem = pl.BlockSpec(memory_space=pltpu.VMEM)
    anywhere = pl.BlockSpec(memory_space=pl.ANY)
    total_rows = steps * own
    bf16 = jnp.bfloat16
    dma = pltpu.SemaphoreType.DMA
    part = (enc_rows, kv_cols + HEAD)
    return pl.pallas_call(
        functools.partial(main_kernel, dims),
        out_shape=(
            jax.ShapeDtypeStruct((ids.shape[1], features), bf16),
            jax.ShapeDtypeStruct((total_rows, HEADS * HEAD), bf16),
        ),
        in_specs=[
            pl.BlockSpec(memory_space=pltpu.SMEM),
            vmem,
            anywhere,
            vmem,
            anywhere,
            vmem,
            anywhere,
            anywhere,
            anywhere,
            anywhere,
        ],
        out_specs=(vmem, vmem),
        scratch_shapes=[
            pltpu.VMEM(hidden.shape, bf16),
            pltpu.VMEM(weight.shape, bf16),
            pltpu.VMEM(table.shape, bf16),
            pltpu.VMEM(part, jnp.float32),
            pltpu.VMEM((narrow - 1,) + part, jnp.float32),
            pltpu.VMEM((slots, features), bf16),
            pltpu.VMEM((ids.shape[1], slots), bf16),
            pltpu.VMEM((total_rows, slots), bf16),
            pltpu.VMEM((wide * enc_rows, kv_cols), bf16),
            pltpu.VMEM((wide // problems * enc_rows, kv_cols), bf16),
            pltpu.VMEM((slots, features), bf16),
            pltpu.VMEM((narrow, slots, features), bf16),
            pltpu.VMEM((slots, kv_cols), bf16),
            pltpu.VMEM(cache.shape, bf16),
            pltpu.VMEM((total_rows, kv_cols), jnp.float32),
            pltpu.VMEM((HEADS * total_rows, HEAD), jnp.float32),
            pltpu.VMEM((HEADS * total_rows, HEAD), jnp.float32),
            dma((6,)),
            dma((narrow - 1,)),
            dma((narrow - 1,)),
            dma((levels,)),
            dma((levels,)),
            dma((wide,)),
            dma((wide,)),
            dma((wide,)),
            dma((wide,)),
            dma((chunks, wide)),
            dma((chunks, wide)),
            dma((narrow - 1, wide)),
            dma((narrow - 1, wide)),
        ],
        compiler_params=pltpu.CompilerParams(
            collective_id=1, has_side_effects=True, vmem_limit_bytes=56 * 2**20
        ),
    )(problem, ids, hidden, gain, weight, picked, table, self_rows, kv_rows, cache)


def hand_over_kernel(count, *refs):
    ins, outs, holds, sems = refs[:count], refs[count : 2 * count], refs[2 * count : -1], refs[-1]
    loads = [pltpu.make_async_copy(ins[k], holds[k], sems.at[0, k]) for k in range(count)]
    stores = [pltpu.make_async_copy(holds[k], outs[k], sems.at[1, k]) for k in range(count)]
    for copy in loads:
        copy.start()
    for load, store in zip(loads, stores):
        load.wait()
        store.start()
    for copy in stores:
        copy.wait()


def hand_over(arrays):
    count = len(arrays)
    anywhere = pl.BlockSpec(memory_space=pl.ANY)
    return pl.pallas_call(
        functools.partial(hand_over_kernel, count),
        out_shape=tuple(jax.ShapeDtypeStruct(array.shape, array.dtype) for array in arrays),
        in_specs=[anywhere] * count,
        out_specs=(anywhere,) * count,
        scratch_shapes=[pltpu.VMEM(array.shape, array.dtype) for array in arrays]
        + [pltpu.SemaphoreType.DMA((2, count))],
    )(*arrays)


def body(
    enc_hidden,
    enc_gain,
    cross_weight,
    assign,
    token_ids,
    cross_table,
    self_table,
    kv_table,
    self_cache,
):
    wide = lax.axis_size("wide")
    narrow = lax.axis_size("narrow")
    steps, cand = token_ids.shape[1:]
    rows = steps * cand
    own = cand // narrow
    per_owner = cross_table.shape[0]
    capacity = max(TILE_ROWS, 2 * rows // wide)
    ids = jnp.broadcast_to(token_ids.reshape(1, rows), (8, rows))
    picked = pick(ids, per_owner, capacity, wide)

    def lookup(table):
        return jnp.dot(picked, table, preferred_element_type=jnp.float32).astype(jnp.bfloat16)

    problems = wide * enc_hidden.shape[0] // ENC_LEN
    chunks = most_parts(cross_table.shape[1] // HEAD)
    cross, selfs = attend(
        assign,
        ids,
        enc_hidden,
        enc_gain.reshape(1, -1),
        cross_weight,
        picked,
        cross_table,
        lookup(self_table),
        lookup(kv_table),
        self_cache[0],
        (wide, narrow, steps, own, problems, chunks),
    )
    cross, selfs = hand_over([cross, selfs])
    return (
        cross.reshape(1, steps, cand, cross.shape[1]),
        selfs.reshape(1, steps, own, HEADS * HEAD),
    )


def solution(mesh):
    placed = (
        P("wide", "narrow"),
        P("narrow"),
        P("narrow", None),
        P("wide"),
        P("wide", None, None),
        P("wide", "narrow"),
        P("wide", "narrow"),
        P("wide", None),
        P("wide", "narrow", None, None),
    )
    return jax.shard_map(
        body,
        mesh=mesh,
        in_specs=placed,
        out_specs=(P("wide", None, None, "narrow"), P("wide", None, "narrow", None)),
        check_vma=False,
    )
```
